32 devices in a mesh: row: 4 (over z), col: 4 (over y, x), tm: 2 (over core).
Axes of the slice: x: 2, y: 2, z: 4, core: 2. Of those that a mesh axis runs over, the one named last changes fastest.
Arguments:
- g_occ: float32 [2, 6144, 6144], P('tm', 'row', 'col'), may hold values from -6 to 6
- g_emp: float32 [2, 6144, 6144], P('tm', 'row', 'col'), may hold values from -6 to 6
- basis: float32 [6144, 1024], P('col'), may hold values from -0.078125 to 0.078125
Outputs:
- spectrum: float32 [2, 1024, 1024], P('tm', 'row', 'col')
The draws below stay inside these ranges and needn't reach their ends.
All inputs are finite; a program needn't handle non-finite values.
Results may differ from the reference program's by a relative error of at most 0.000071.
Values sent between devices are 32-bit elements; how exact they have to be, the bound alone decides.
No kernel may reach another device: no remote copies, remote signals or barrier semaphores. Data moves between devices by JAX's collectives and lax.ppermute only.
A program may use at most 128 MiB of HBM per device.

```python
import jax
import jax.numpy as jnp
from jax import lax

NG = 6144
AUX = 1024
TAU = 2


def level_of(stream_key, extent, cuts, low, top_value):
    gain, own = 1.0, jax.random.fold_in(stream_key, 6)
    for axis_at, shards_of in cuts:
        steps = jnp.exp(jax.random.uniform(jax.random.fold_in(own, axis_at), (shards_of,), jnp.float32, low / len(cuts), top_value / len(cuts)))
        gain = gain * jnp.repeat(steps, extent[axis_at] // shards_of).reshape([-1 if axis == axis_at else 1 for axis in range(len(extent))])
    return gain


def scatter_about(rng, dims, scale, bound, pieces=(), kind=jnp.bfloat16):
    drawn = jax.random.normal(rng, dims, jnp.float32) * scale
    if len(pieces) > 0:
        drawn = level_of(rng, dims, pieces, -0.22, 0.18) * drawn
    return jnp.clip(drawn, min=-bound, max=bound).astype(kind)


def setup_inputs(seed: int = 0) -> dict:
    keys = jax.random.split(jax.random.key(seed), 4)
    return {
        "g_occ": scatter_about(keys[0], (TAU, NG, NG), 1.0, 6.0, ((0, 2), (1, 4), (2, 4)), jnp.float32),
        "g_emp": scatter_about(keys[1], (TAU, NG, NG), 1.0, 6.0, ((0, 2), (1, 4), (2, 4)), jnp.float32),
        "basis": scatter_about(keys[2], (NG, AUX), NG ** -0.5, 0.078125, ((0, 4),), jnp.float32),
    }


HIGHEST_PRECISION = lax.Precision.HIGHEST

def cosine_table(points):
    orders = jnp.arange(points, dtype=jnp.float32)[:, None]
    moments = jnp.arange(points, dtype=jnp.float32)[None, :]
    return jnp.sqrt(2.0 / points) * jnp.cos(jnp.pi * (orders + 0.5) * (moments + 0.5) / points)

def reference(g_occ, g_emp, basis):

    def project(green_pair):
        response = green_pair[0] * green_pair[1]
        right_side = jnp.dot(response, basis, precision=HIGHEST_PRECISION, preferred_element_type=jnp.float32)
        return lax.dot_general(basis, right_side, (((0,), (0,)), ((), ())), precision=HIGHEST_PRECISION, preferred_element_type=jnp.float32)
    blocks = lax.map(project, (g_occ, g_emp))
    cosines = cosine_table(TAU)
    return jnp.einsum('kt,tab->kab', cosines, blocks, precision=HIGHEST_PRECISION)
```

```python
import jax
import jax.numpy as jnp
from jax import lax
from jax.experimental import pallas as pl
from jax.experimental.pallas import tpu as pltpu
from jax.sharding import PartitionSpec as P


HIGHEST_PRECISION = lax.Precision.HIGHEST
AXES = ("row", "col", "tm")
F32 = jnp.float32
THREE_PASSES = lax.Precision.HIGH


def broadcast(block, axis, source):
    block = jnp.where(lax.axis_index(axis) == source, block, jnp.zeros_like(block))
    return lax.psum(block, axis)


def cosine_weights(points, orders):
    moment = lax.axis_index("tm").astype(F32)
    return jnp.sqrt(2.0 / points) * jnp.cos(jnp.pi * (orders + 0.5) * (moment + 0.5) / points)


def general(g_occ, g_emp, basis):
    response = g_occ[0] * g_emp[0]
    rows_dev = response.shape[0]
    cols_dev = basis.shape[0]
    first_row = lax.axis_index("row") * rows_dev
    owner = first_row // cols_dev
    offset_local = first_row % cols_dev
    mine = lax.dynamic_slice_in_dim(basis, offset_local, rows_dev, 0)
    panel = broadcast(mine, "col", owner)
    mixed = jnp.dot(
        response, basis, precision=HIGHEST_PRECISION, preferred_element_type=F32
    )
    mixed_rows = lax.psum_scatter(mixed, "col", scatter_dimension=1, tiled=True)
    projected = lax.psum_scatter(
        lax.dot_general(
            panel,
            mixed_rows,
            (((0,), (0,)), ((), ())),
            precision=HIGHEST_PRECISION,
            preferred_element_type=F32,
        ),
        "row",
        scatter_dimension=0,
        tiled=True,
    )
    points = lax.axis_size("tm")
    orders = jnp.arange(points, dtype=jnp.int32).astype(F32)
    weights = cosine_weights(points, orders)
    return lax.psum_scatter(
        weights[:, None, None] * projected[None, :, :], "tm", scatter_dimension=0, tiled=True
    )


def accumulate(ref, value):
    @pl.when(pl.program_id(0) == 0)
    def _():
        ref[...] = value

    @pl.when(pl.program_id(0) > 0)
    def _():
        ref[...] += value


def mix_kernel(at_ref, occ_ref, emp_ref, basis_ref, *refs):
    response = occ_ref[...] * emp_ref[...]
    accumulate(refs[-1], jnp.dot(response, basis_ref[...], precision=THREE_PASSES, preferred_element_type=F32))


def mix(at, piece, tall, occ, emp, basis, held):
    rows, inner = occ.shape
    aux = basis.shape[1]
    deep = inner // 3
    unit = rows // 4
    source = pl.BlockSpec((tall, deep), lambda k, at: (at[piece * tall // unit] * unit // tall, k))
    return pl.pallas_call(
        mix_kernel,
        grid_spec=pltpu.PrefetchScalarGridSpec(
            num_scalar_prefetch=1,
            grid=(inner // deep,),
            in_specs=[source, source, pl.BlockSpec((deep, aux), lambda k, at: (k, 0))]
            + [pl.BlockSpec(memory_space=pl.ANY)] * len(held),
            out_specs=pl.BlockSpec((tall, aux), lambda k, at: (piece, 0)),
        ),
        out_shape=jax.ShapeDtypeStruct((rows, aux), F32),
        input_output_aliases={4: 0} if held else {},
        cost_estimate=pl.CostEstimate(
            flops=6 * tall * inner * aux,
            bytes_accessed=8 * tall * inner + 4 * basis.size + 4 * tall * aux,
            transcendentals=0,
        ),
        name="mix",
    )(at, occ, emp, basis, *held)


def project_kernel(at_ref, *refs):
    panels, mixed_ref, outs, sum_ref = refs[:4], refs[4], refs[5:-1], refs[-1]
    steps = pl.num_programs(0)
    for k in range(2):

        @pl.when(pl.program_id(0) == k)
        def _():
            panel = jnp.concatenate([ref[...] for ref in panels[2 * k : 2 * k + 2]])
            value = lax.dot_general(
                panel, mixed_ref[...], (((0,), (0,)), ((), ())), precision=THREE_PASSES, preferred_element_type=F32
            )
            if k == 0:
                sum_ref[...] = value
            else:
                sum_ref[...] += value

    @pl.when(pl.program_id(0) == steps - 1)
    def _():
        wide = outs[0].shape[1]
        for k, out in enumerate(outs):
            out[...] = sum_ref[:, pl.ds(pl.multiple_of(at_ref[4 + k] * wide, wide), wide)]


def project(at, panels, mixed):
    tall, wide = panels[0].shape
    rows, aux = mixed.shape
    panel = pl.BlockSpec((tall, wide), lambda k, at: (0, 0))
    return pl.pallas_call(
        project_kernel,
        grid_spec=pltpu.PrefetchScalarGridSpec(
            num_scalar_prefetch=1,
            grid=(2,),
            in_specs=[panel] * 4 + [pl.BlockSpec((2 * tall, aux), lambda k, at: (k, 0))],
            out_specs=[pl.BlockSpec((wide, aux // 4), lambda k, at: (0, 0))] * 4,
            scratch_shapes=[pltpu.VMEM((wide, aux), F32)],
        ),
        out_shape=[jax.ShapeDtypeStruct((wide, aux // 4), F32)] * 4,
        cost_estimate=pl.CostEstimate(
            flops=6 * wide * rows * aux,
            bytes_accessed=4 * rows * (wide + aux) + 4 * wide * aux,
            transcendentals=0,
        ),
        name="project",
    )(at, *panels, mixed)


def permute(x, pair):
    pairs = []
    sizes = [lax.axis_size(a) for a in AXES]
    for r in range(sizes[0]):
        for c in range(sizes[1]):
            for t in range(sizes[2]):
                to = pair(r, c, t)
                if to is not None:
                    pairs.append(tuple((a * sizes[1] + b) * sizes[2] + d for a, b, d in ((r, c, t), to)))
    return lax.ppermute(x, AXES, pairs)


RING = ((0, 1, 3, 2), (0, 2, 3, 1))


def along_ring(first, last):
    def pair(r, c, t):
        hop = RING[t].index(r ^ c)
        return (r, r ^ RING[t][hop + 1], t) if first <= hop <= last and hop < 3 else None

    return pair


def per_device(g_occ, g_emp, basis):
    occ, emp = g_occ[0], g_emp[0]
    row, col, core = (lax.axis_index(a) for a in AXES)
    rows, aux = basis.shape
    tall, wide = rows // 4, aux // 4
    chunks = (0, 3, 1, 2)

    quarter = [2 * core, 2 * core + 1, 2 - 2 * core, 3 - 2 * core]
    at = jnp.stack(quarter + [col ^ k for k in range(4)]).astype(jnp.int32)

    xor = row ^ col
    place = jnp.where(core == 0, jnp.where(xor == 3, 2, jnp.where(xor == 2, 3, xor)),
                      jnp.where(xor == 2, 1, jnp.where(xor == 3, 2, jnp.where(xor == 1, 3, xor))))

    def own(source, s, i):
        return lax.dynamic_slice(source, (quarter[s] * tall, chunks[i] * wide), (tall, wide))

    got = [[], []]
    for step in range(6):
        for s in range(2):
            if step == 0:
                out = own(lax.optimization_barrier(basis), s, 0)
            else:
                out = got[s][-1]
                if step < 4:
                    source, out = lax.optimization_barrier((basis, out))
                    out = jnp.where(place == 0, own(source, s, step), out)
            got[s].append(permute(out, along_ring(max(0, step - 3), min(2, step))))

    held = ()
    for piece, high in ((0, 2 * tall), (2, tall), (3, tall)):
        held = (mix(at, piece, high, occ, emp, basis, held),)
    (mixed,) = held

    def swap(x):
        return permute(x, lambda r, c, t: (r, c, 1 - t))

    sums = []
    gate = ()
    for i, j in enumerate(chunks):
        mine = []
        for s in range(2):
            source, seen, gate = lax.optimization_barrier((basis, got[s][i : i + 3], gate))
            mine.append(jnp.where(place == 0, own(source, s, i),
                                  jnp.where(place == 1, seen[0], jnp.where(place == 2, seen[1], seen[2]))))
        other = [swap(mine[s]) for s in range(2)]
        gate = tuple(other)
        parts = project(at, mine + other, mixed)
        total = parts[0]
        for k in (1, 2, 3):
            total = total + permute(parts[k], lambda r, c, t: (r, c ^ k, t))
        whole = total
        for k in (1, 2, 3):
            whole = whole + permute(total, lambda r, c, t: (j, c, t) if r ^ k == j else None)
        sums.append((j, whole))

    mine = sums[0][1]
    for j, part in sums[1:]:
        mine = jnp.where(row == j, part, mine)
    other = swap(mine)
    order = core.astype(F32)
    points = lax.axis_size("tm")

    def weight(moment):
        return jnp.sqrt(2.0 / points) * jnp.cos(jnp.pi * (order + 0.5) * (moment + 0.5) / points)

    return (weight(order) * mine + weight(1 - order) * other)[None]


def solution(mesh):
    sizes = [mesh.shape[a] for a in AXES]
    special = sizes == [4, 4, 2]

    def body(g_occ, g_emp, basis):
        fits = special and g_occ.shape[1] == basis.shape[0] and not basis.shape[0] % 128 and not basis.shape[1] % 512
        return (per_device if fits else general)(g_occ, g_emp, basis)

    return jax.shard_map(
        body,
        mesh=mesh,
        in_specs=(P("tm", "row", "col"), P("tm", "row", "col"), P("col", None)),
        out_specs=P("tm", "row", "col"),
        check_vma=False,
    )
```

```python
import functools

import jax
import jax.numpy as jnp
from jax import lax
from jax.experimental import pallas as pl
from jax.experimental.pallas import tpu as pltpu
from jax.sharding import PartitionSpec as P


HIGHEST_PRECISION = lax.Precision.HIGHEST
AXES = ("row", "col", "tm")
F32 = jnp.float32
THREE_PASSES = lax.Precision.HIGH
MIX_VMEM = 24 << 20
PROJECT_VMEM = 20 << 20


def broadcast(block, axis, source):
    block = jnp.where(lax.axis_index(axis) == source, block, jnp.zeros_like(block))
    return lax.psum(block, axis)


def cosine_weights(points, orders):
    moment = lax.axis_index("tm").astype(F32)
    return jnp.sqrt(2.0 / points) * jnp.cos(jnp.pi * (orders + 0.5) * (moment + 0.5) / points)


def general(g_occ, g_emp, basis):
    response = g_occ[0] * g_emp[0]
    rows_dev = response.shape[0]
    cols_dev = basis.shape[0]
    first_row = lax.axis_index("row") * rows_dev
    owner = first_row // cols_dev
    offset_local = first_row % cols_dev
    mine = lax.dynamic_slice_in_dim(basis, offset_local, rows_dev, 0)
    panel = broadcast(mine, "col", owner)
    mixed = jnp.dot(
        response, basis, precision=HIGHEST_PRECISION, preferred_element_type=F32
    )
    mixed_rows = lax.psum_scatter(mixed, "col", scatter_dimension=1, tiled=True)
    projected = lax.psum_scatter(
        lax.dot_general(
            panel,
            mixed_rows,
            (((0,), (0,)), ((), ())),
            precision=HIGHEST_PRECISION,
            preferred_element_type=F32,
        ),
        "row",
        scatter_dimension=0,
        tiled=True,
    )
    points = lax.axis_size("tm")
    orders = jnp.arange(points, dtype=jnp.int32).astype(F32)
    weights = cosine_weights(points, orders)
    return lax.psum_scatter(
        weights[:, None, None] * projected[None, :, :], "tm", scatter_dimension=0, tiled=True
    )


def mix_kernel(occ_ref, emp_ref, basis_ref, mixed_ref):
    step = pl.program_id(0)
    deep = occ_ref.shape[1]
    response = occ_ref[...] * emp_ref[...]
    part = basis_ref[pl.ds(pl.multiple_of(step * deep, deep), deep), :]
    value = jnp.dot(response, part, precision=THREE_PASSES, preferred_element_type=F32)

    @pl.when(step == 0)
    def _():
        mixed_ref[...] = value

    @pl.when(step > 0)
    def _():
        mixed_ref[...] += value


def mix(piece, tall, occ, emp, basis):
    _, inner = occ.shape
    aux = basis.shape[1]
    deep = inner // 3
    source = pl.BlockSpec((tall, deep), lambda k: (piece, k))
    return pl.pallas_call(
        mix_kernel,
        grid=(inner // deep,),
        in_specs=[source, source, pl.BlockSpec(memory_space=pltpu.VMEM)],
        out_specs=pl.BlockSpec((tall, aux), lambda k: (0, 0)),
        out_shape=jax.ShapeDtypeStruct((tall, aux), F32),
        cost_estimate=pl.CostEstimate(
            flops=6 * tall * inner * aux,
            bytes_accessed=8 * tall * inner + 4 * basis.size + 4 * tall * aux,
            transcendentals=0,
        ),
        compiler_params=pltpu.CompilerParams(vmem_limit_bytes=MIX_VMEM),
        name="mix",
    )(*(pltpu.with_memory_space_constraint(x, pltpu.HBM) for x in (occ, emp)), basis)


def project_kernel(groups, count, *refs):
    panels, mixed, outs, panel_ref, sum_ref = refs[:4], refs[4 : 4 + count], refs[4 + count : -2], refs[-2], refs[-1]
    tall = panels[0].shape[0]
    for i, ref in enumerate(panels):
        half = lax.axis_index("tm") if i < 2 else 1 - lax.axis_index("tm")
        panel_ref[pl.ds(pl.multiple_of((2 * half + i % 2) * tall, tall), tall), :] = ref[...]
    deep = mixed[0].shape[0]
    for k, ref in enumerate(mixed):
        value = lax.dot_general(
            panel_ref[k * deep : (k + 1) * deep, :],
            ref[...],
            (((0,), (0,)), ((), ())),
            precision=THREE_PASSES,
            preferred_element_type=F32,
        )
        if k == 0:
            sum_ref[...] = value
        else:
            sum_ref[...] += value
    wide = outs[0].shape[-1]

    def part(k):
        return sum_ref[:, pl.ds(pl.multiple_of((lax.axis_index("col") ^ k) * wide, wide), wide)]

    for group, out in zip(groups, outs):
        if isinstance(group, int):
            out[...] = part(group)
        else:
            for i, k in enumerate(group):
                out[i] = part(k)


def project(panels, mixed, groups):
    tall, wide = panels[0].shape
    aux = mixed[0].shape[1]
    block = (wide, aux // 4)
    whole = pl.BlockSpec(memory_space=pltpu.VMEM)
    shapes = [jax.ShapeDtypeStruct(block if isinstance(g, int) else (len(g), *block), F32) for g in groups]
    return pl.pallas_call(
        functools.partial(project_kernel, groups, len(mixed)),
        in_specs=[whole] * (4 + len(mixed)),
        out_specs=[whole] * len(shapes),
        scratch_shapes=[pltpu.VMEM((4 * tall, wide), F32), pltpu.VMEM((wide, aux), F32)],
        out_shape=shapes,
        cost_estimate=pl.CostEstimate(
            flops=24 * wide * tall * aux,
            bytes_accessed=16 * tall * (wide + aux) + 4 * wide * aux,
            transcendentals=0,
        ),
        compiler_params=pltpu.CompilerParams(vmem_limit_bytes=PROJECT_VMEM),
        name="project",
    )(*panels, *mixed)


def permute(x, pair):
    pairs = []
    sizes = [lax.axis_size(a) for a in AXES]
    for r in range(sizes[0]):
        for c in range(sizes[1]):
            for t in range(sizes[2]):
                to = pair(r, c, t)
                if to is not None:
                    pairs.append(tuple((a * sizes[1] + b) * sizes[2] + d for a, b, d in ((r, c, t), to)))
    return lax.ppermute(x, AXES, pairs)


RING = ((0, 1, 3, 2), (0, 2, 3, 1))


def along_ring(first, last):
    def pair(r, c, t):
        hop = RING[t].index(r ^ c)
        return (r, r ^ RING[t][hop + 1], t) if first <= hop <= last and hop < 3 else None

    return pair


def per_device(g_occ, g_emp, basis):
    occ, emp = g_occ[0], g_emp[0]
    row, col, core = (lax.axis_index(a) for a in AXES)
    rows, aux = basis.shape
    tall, wide = rows // 4, aux // 4
    chunks = (0, 3, 1, 2)

    quarter = [2 * core, 2 * core + 1, 2 - 2 * core, 3 - 2 * core]

    xor = row ^ col
    place = jnp.where(core == 0, jnp.where(xor == 3, 2, jnp.where(xor == 2, 3, xor)),
                      jnp.where(xor == 2, 1, jnp.where(xor == 3, 2, jnp.where(xor == 1, 3, xor))))

    def own(source, s, i):
        return lax.dynamic_slice(source, (quarter[s] * tall, chunks[i] * wide), (tall, wide))

    got = [[], []]
    for step in range(6):
        for s in range(2):
            if step == 0:
                out = own(lax.optimization_barrier(basis), s, 0)
            else:
                out = got[s][-1]
                if step < 4:
                    source, out = lax.optimization_barrier((basis, out))
                    out = jnp.where(place == 0, own(source, s, step), out)
            got[s].append(permute(out, along_ring(max(0, step - 3), min(2, step))))

    mixed = []
    for piece in range(3):
        mixed.append(mix(piece, rows // 3, occ, emp, basis))

    def swap(x):
        return permute(x, lambda r, c, t: (r, c, 1 - t))

    sums, wholes = [], []
    gate = ()
    for i, j in enumerate(chunks):
        source, seen, gate = lax.optimization_barrier((basis, [got[s][i : i + 3] for s in range(2)], gate))
        mine = [
            jnp.where(place == 0, own(source, s, i),
                      jnp.where(place == 1, seen[s][0], jnp.where(place == 2, seen[s][1], seen[s][2])))
            for s in range(2)
        ]
        other = [swap(mine[s]) for s in range(2)]
        gate = tuple(other)
        parts = project(mine + other, mixed, ((0, 2), (1, 3)) if i in (0, 2) else ((0, 1), (2, 3)) if i == 1 else (0, 1, 2, 3))
        if i < len(chunks) - 1:
            first, second = (1, 2) if i % 2 == 0 else (2, 1)
            near = parts[0] + permute(parts[1], lambda r, c, t: (r, c ^ first, t))
            total = near[0] + permute(near[1], lambda r, c, t: (r, c ^ second, t))
        else:
            total = parts[0]
            for k in (1, 2, 3):
                total = total + permute(parts[k], lambda r, c, t: (r, c ^ k, t))
        sums.append(total)
        if i % 2:
            here = chunks[i - 1]
            pair = sums[-2:]

            def pick(k):
                return jnp.where(row ^ k == here, pair[0], pair[1])

            whole = pick(0)
            for k in (1, 2, 3):
                whole = whole + permute(
                    pick(k), lambda r, c, t: (r ^ k, c, t) if r ^ k in chunks[i - 1 : i + 1] else None
                )
            wholes.append(whole)

    mine = jnp.where((row == chunks[0]) | (row == chunks[1]), wholes[0], wholes[1])
    other = swap(mine)
    order = core.astype(F32)
    points = lax.axis_size("tm")

    def weight(moment):
        return jnp.sqrt(2.0 / points) * jnp.cos(jnp.pi * (order + 0.5) * (moment + 0.5) / points)

    return (weight(order) * mine + weight(1 - order) * other)[None]


def solution(mesh):
    sizes = [mesh.shape[a] for a in AXES]
    special = sizes == [4, 4, 2]

    def body(g_occ, g_emp, basis):
        fits = special and g_occ.shape[1] == basis.shape[0] and not basis.shape[0] % 384 and not basis.shape[1] % 512
        return (per_device if fits else general)(g_occ, g_emp, basis)

    return jax.shard_map(
        body,
        mesh=mesh,
        in_specs=(P("tm", "row", "col"), P("tm", "row", "col"), P("col", None)),
        out_specs=P("tm", "row", "col"),
        check_vma=False,
    )
```

```python
import functools

import jax
import jax.numpy as jnp
from jax import lax
from jax.experimental import pallas as pl
from jax.experimental.pallas import tpu as pltpu
from jax.sharding import PartitionSpec as P


HIGHEST_PRECISION = lax.Precision.HIGHEST
AXES = ("row", "col", "tm")
F32 = jnp.float32
THREE_PASSES = lax.Precision.HIGH
MIX_VMEM = 24 << 20
PROJECT_VMEM = 20 << 20


def broadcast(block, axis, source):
    block = jnp.where(lax.axis_index(axis) == source, block, jnp.zeros_like(block))
    return lax.psum(block, axis)


def cosine_weights(points, orders):
    moment = lax.axis_index("tm").astype(F32)
    return jnp.sqrt(2.0 / points) * jnp.cos(jnp.pi * (orders + 0.5) * (moment + 0.5) / points)


def general(g_occ, g_emp, basis):
    response = g_occ[0] * g_emp[0]
    rows_dev = response.shape[0]
    cols_dev = basis.shape[0]
    first_row = lax.axis_index("row") * rows_dev
    owner = first_row // cols_dev
    offset_local = first_row % cols_dev
    mine = lax.dynamic_slice_in_dim(basis, offset_local, rows_dev, 0)
    panel = broadcast(mine, "col", owner)
    mixed = jnp.dot(
        response, basis, precision=HIGHEST_PRECISION, preferred_element_type=F32
    )
    mixed_rows = lax.psum_scatter(mixed, "col", scatter_dimension=1, tiled=True)
    projected = lax.psum_scatter(
        lax.dot_general(
            panel,
            mixed_rows,
            (((0,), (0,)), ((), ())),
            precision=HIGHEST_PRECISION,
            preferred_element_type=F32,
        ),
        "row",
        scatter_dimension=0,
        tiled=True,
    )
    points = lax.axis_size("tm")
    orders = jnp.arange(points, dtype=jnp.int32).astype(F32)
    weights = cosine_weights(points, orders)
    return lax.psum_scatter(
        weights[:, None, None] * projected[None, :, :], "tm", scatter_dimension=0, tiled=True
    )


def mix_kernel(occ_ref, emp_ref, basis_ref, mixed_ref):
    step = pl.program_id(0)
    deep = occ_ref.shape[1]
    response = occ_ref[...] * emp_ref[...]
    part = basis_ref[...]
    if basis_ref.shape[0] != deep:
        part = basis_ref[pl.ds(pl.multiple_of(step * deep, deep), deep), :]
    value = jnp.dot(response, part, precision=THREE_PASSES, preferred_element_type=F32)

    @pl.when(step == 0)
    def _():
        mixed_ref[...] = value

    @pl.when(step > 0)
    def _():
        mixed_ref[...] += value


def in_hbm(x):
    return pltpu.with_memory_space_constraint(x, pltpu.HBM)


def mix(piece, tall, occ, emp, basis, streamed):
    _, inner = occ.shape
    aux = basis.shape[1]
    deep = inner // 3
    source = pl.BlockSpec((tall, deep), lambda k: (piece, k))
    return pl.pallas_call(
        mix_kernel,
        grid=(inner // deep,),
        in_specs=[source, source, pl.BlockSpec((deep, aux), lambda k: (k, 0)) if streamed else pl.BlockSpec(memory_space=pltpu.VMEM)],
        out_specs=pl.BlockSpec((tall, aux), lambda k: (0, 0)),
        out_shape=jax.ShapeDtypeStruct((tall, aux), F32),
        cost_estimate=pl.CostEstimate(
            flops=6 * tall * inner * aux,
            bytes_accessed=8 * tall * inner + 4 * basis.size + 4 * tall * aux,
            transcendentals=0,
        ),
        compiler_params=pltpu.CompilerParams(vmem_limit_bytes=MIX_VMEM),
        name="mix",
    )(in_hbm(occ), in_hbm(emp), in_hbm(basis) if streamed else basis)


def project_kernel(groups, count, *refs):
    panels, mixed, outs, panel_ref, sum_ref = refs[:4], refs[4 : 4 + count], refs[4 + count : -2], refs[-2], refs[-1]
    tall = panels[0].shape[0]
    for i, ref in enumerate(panels):
        half = lax.axis_index("tm") if i < 2 else 1 - lax.axis_index("tm")
        panel_ref[pl.ds(pl.multiple_of((2 * half + i % 2) * tall, tall), tall), :] = ref[...]
    deep = mixed[0].shape[0]
    for k, ref in enumerate(mixed):
        value = lax.dot_general(
            panel_ref[k * deep : (k + 1) * deep, :],
            ref[...],
            (((0,), (0,)), ((), ())),
            precision=THREE_PASSES,
            preferred_element_type=F32,
        )
        if k == 0:
            sum_ref[...] = value
        else:
            sum_ref[...] += value
    wide = outs[0].shape[-1]

    def part(k):
        return sum_ref[:, pl.ds(pl.multiple_of((lax.axis_index("col") ^ k) * wide, wide), wide)]

    for group, out in zip(groups, outs):
        if isinstance(group, int):
            out[...] = part(group)
        else:
            for i, k in enumerate(group):
                out[i] = part(k)


def project(panels, mixed, groups):
    tall, wide = panels[0].shape
    aux = mixed[0].shape[1]
    block = (wide, aux // 4)
    whole = pl.BlockSpec(memory_space=pltpu.VMEM)
    shapes = [jax.ShapeDtypeStruct(block if isinstance(g, int) else (len(g), *block), F32) for g in groups]
    return pl.pallas_call(
        functools.partial(project_kernel, groups, len(mixed)),
        in_specs=[whole] * (4 + len(mixed)),
        out_specs=[whole] * len(shapes),
        scratch_shapes=[pltpu.VMEM((4 * tall, wide), F32), pltpu.VMEM((wide, aux), F32)],
        out_shape=shapes,
        cost_estimate=pl.CostEstimate(
            flops=24 * wide * tall * aux,
            bytes_accessed=16 * tall * (wide + aux) + 4 * wide * aux,
            transcendentals=0,
        ),
        compiler_params=pltpu.CompilerParams(vmem_limit_bytes=PROJECT_VMEM),
        name="project",
    )(*panels, *mixed)


def pick_kernel(dests, count, *refs):
    terms, outs = refs[:-4], refs[-4:]
    totals = []
    for part in (terms[:count], terms[count:]):
        total = part[0][...]
        for ref in part[1:]:
            total = total + (ref[0] if len(ref.shape) == 3 else ref[...])
        totals.append(total)
    for k, out in enumerate(outs):
        out[...] = jnp.where(lax.axis_index("row") ^ k == dests[0], *totals)


def pick(dests, one, two):
    whole = pl.BlockSpec(memory_space=pltpu.VMEM)
    shape = jax.ShapeDtypeStruct(one[0].shape, F32)
    return pl.pallas_call(
        functools.partial(pick_kernel, dests, len(one)),
        in_specs=[whole] * (len(one) + len(two)),
        out_specs=[whole] * 4,
        out_shape=[shape] * 4,
        cost_estimate=pl.CostEstimate(flops=0, bytes_accessed=40 * one[0].size, transcendentals=0),
        compiler_params=pltpu.CompilerParams(vmem_limit_bytes=PROJECT_VMEM),
        name="pick",
    )(*one, *two)


def permute(x, pair):
    pairs = []
    sizes = [lax.axis_size(a) for a in AXES]
    for r in range(sizes[0]):
        for c in range(sizes[1]):
            for t in range(sizes[2]):
                to = pair(r, c, t)
                if to is not None:
                    pairs.append(tuple((a * sizes[1] + b) * sizes[2] + d for a, b, d in ((r, c, t), to)))
    return lax.ppermute(x, AXES, pairs)


RING = ((0, 1, 3, 2), (0, 2, 3, 1))


def along_ring(first, last):
    def pair(r, c, t):
        hop = RING[t].index(r ^ c)
        return (r, r ^ RING[t][hop + 1], t) if first <= hop <= last and hop < 3 else None

    return pair


def per_device(g_occ, g_emp, basis):
    occ, emp = g_occ[0], g_emp[0]
    row, col, core = (lax.axis_index(a) for a in AXES)
    rows, aux = basis.shape
    tall, wide = rows // 4, aux // 4
    chunks = (0, 3, 1, 2)
    hops = (2, 1, 1, 1)

    quarter = [2 * core, 2 * core + 1, 2 - 2 * core, 3 - 2 * core]

    xor = row ^ col
    place = jnp.where(core == 0, jnp.where(xor == 3, 2, jnp.where(xor == 2, 3, xor)),
                      jnp.where(xor == 2, 1, jnp.where(xor == 3, 2, jnp.where(xor == 1, 3, xor))))

    def own(source, s, i):
        return lax.dynamic_slice(source, (quarter[s] * tall, chunks[i] * wide), (tall, wide))

    got = [[], []]
    for step in range(6):
        for s in range(2):
            if step == 0:
                out = own(lax.optimization_barrier(basis), s, 0)
            else:
                out = got[s][-1]
                source, out = lax.optimization_barrier((basis, out))
                out = jnp.where(place == 0, own(source, s, min(step, 3)), out)
            got[s].append(permute(out, along_ring(max(0, step - 3), min(2, step))))

    mixed = []
    for piece in range(3):
        mixed.append(mix(piece, rows // 3, occ, emp, basis, streamed=piece == 0))

    def swap(x):
        return permute(x, lambda r, c, t: (r, c, 1 - t))

    sums, wholes = [], []
    gate = ()
    for i, j in enumerate(chunks):
        source, seen, gate = lax.optimization_barrier((basis, [got[s][i : i + 3] for s in range(2)], gate))
        mine = [
            jnp.where(place == 0, own(source, s, i),
                      jnp.where(place == 1, seen[s][0], jnp.where(place == 2, seen[s][1], seen[s][2])))
            for s in range(2)
        ]
        other = [swap(mine[s]) for s in range(2)]
        gate = tuple(other)
        groups = (0, 1, 2, 3) if hops[i] == 1 else (0, 2, (1, 3)) if i % 2 == 0 else (0, 1, (2, 3))
        parts = project(mine + other, mixed, groups)
        if hops[i] == 2:
            first, second = (1, 2) if i % 2 == 0 else (2, 1)
            came = permute(parts[2], lambda r, c, t: (r, c ^ first, t))
            terms = [parts[0], came, permute(parts[1] + came[1], lambda r, c, t: (r, c ^ second, t))]
        else:
            terms = [parts[0]]
            for k in (1, 2, 3):
                terms.append(permute(parts[k], lambda r, c, t: (r, c ^ k, t)))
        sums.append(terms)
        if i % 2:
            picks = pick(chunks[i - 1 : i + 1], *sums[-2:])
            whole = picks[0]
            for k in (1, 2, 3):
                whole = whole + permute(
                    picks[k], lambda r, c, t: (r ^ k, c, t) if r ^ k in chunks[i - 1 : i + 1] else None
                )
            wholes.append(whole)

    mine = jnp.where((row == chunks[0]) | (row == chunks[1]), wholes[0], wholes[1])
    other = swap(mine)
    order = core.astype(F32)
    points = lax.axis_size("tm")

    def weight(moment):
        return jnp.sqrt(2.0 / points) * jnp.cos(jnp.pi * (order + 0.5) * (moment + 0.5) / points)

    return (weight(order) * mine + weight(1 - order) * other)[None]


def solution(mesh):
    sizes = [mesh.shape[a] for a in AXES]
    special = sizes == [4, 4, 2]

    def body(g_occ, g_emp, basis):
        fits = special and g_occ.shape[1] == basis.shape[0] and not basis.shape[0] % 384 and not basis.shape[1] % 512
        return (per_device if fits else general)(g_occ, g_emp, basis)

    return jax.shard_map(
        body,
        mesh=mesh,
        in_specs=(P("tm", "row", "col"), P("tm", "row", "col"), P("col", None)),
        out_specs=P("tm", "row", "col"),
        check_vma=False,
    )
```
